128 devices in a mesh: row: 16 (over x, z_lo, core), col: 8 (over z_hi, y).
Axes of the slice: x: 4, y: 4, z: 4 (z_hi: 2, z_lo: 2; z = z_hi * 2 + z_lo), core: 2. Of those that a mesh axis runs over, the one named last changes fastest.
Arguments:
- design: float32 [1536, 24576], P(('row', 'col')), may hold values from -6 to 6
- filter_band: float32 [1536, 8], P(('row', 'col')), may hold values from -3 to 3
- arc_lengths: int32 [128, 2], P(('row', 'col')), may hold values from 1 to 11, as said below
Outputs:
- normal: float32 [24576, 24576], P('row', 'col')
The draws below stay inside these ranges and needn't reach their ends.
Inputs may be any that keep to these rules, and one draw needn't show every extreme that they name: `arc_lengths`: row d gives the lengths of the two arcs held in device d's first slots, in slot order; each row sums to between 2 and 12, some row sums to exactly 12, and all rows together sum to 896.
All inputs are finite; a program needn't handle non-finite values.
Results may differ from the reference program's by a relative error of at most 0.000075.
Values sent between devices are 32-bit elements; how exact they have to be, the bound alone decides.
No kernel may reach another device: no remote copies, remote signals or barrier semaphores. Data moves between devices by JAX's collectives and lax.ppermute only.
A program may use at most 128 MiB of HBM per device.

```python
import jax
import jax.numpy as jnp
from jax import lax

P_SIZE = 24576
OBS_DEV = 7
LAGS = 8
CAP = 12
SLOTS = 1536
OBS = 896


def draw_arc_lengths(key, part):
    devices = SLOTS // CAP
    halves = devices // 2
    key_size, key_sign, key_order, key_split = jax.random.split(key, 4)
    spread = jax.random.randint(key_size, (halves,), 0, OBS_DEV - 1)
    spread = spread.at[0].set(OBS_DEV - 2)
    sign_flip = 2 * jax.random.randint(key_sign, (halves,), 0, 2) - 1
    deltas = spread * sign_flip
    paired = jnp.concatenate([OBS_DEV + deltas, OBS_DEV - deltas])
    totals = paired[jax.random.permutation(key_order, devices)]
    first_arc = jax.random.randint(key_split, (devices,), 1, totals)
    first_arc = jnp.where(totals == CAP, CAP - 1, first_arc)
    return jnp.stack([first_arc, totals - first_arc], axis=1).astype(jnp.int32)


def block_scale(rng, dims, cuts, low, top_value):
    gain, own = 1.0, jax.random.fold_in(rng, 6)
    for axis_at, shards_of in cuts:
        draws = jnp.exp(jax.random.uniform(jax.random.fold_in(own, axis_at), (shards_of,), jnp.float32, low / len(cuts), top_value / len(cuts)))
        gain = gain * jnp.repeat(draws, dims[axis_at] // shards_of).reshape([-1 if axis == axis_at else 1 for axis in range(len(dims))])
    return gain


def noise(rng, dims, width, limit, cuts=(), held_as=jnp.bfloat16):
    factor_of = block_scale(rng, dims, cuts, -0.22, 0.18) if cuts else 1.0
    values = jax.random.normal(rng, dims, jnp.float32) * width * factor_of
    return jnp.minimum(jnp.maximum(values, -limit), limit).astype(held_as)


def setup_inputs(seed: int = 0) -> dict:
    key_of = jax.random.split(jax.random.key(seed), 4)
    design = noise(key_of[0], (SLOTS, P_SIZE), 1.0, 6.0, ((0, 128),), jnp.float32)
    filter_band = noise(key_of[1], (SLOTS, LAGS), 0.5, 3.0, ((0, 128),), jnp.float32)
    arc_lengths = draw_arc_lengths(jax.random.fold_in(key_of[3], 71), 0)
    return dict(design=design, filter_band=filter_band, arc_lengths=arc_lengths)


def reference(design, filter_band, arc_lengths):
    first_arc = arc_lengths[:, 0:1]
    filled = first_arc + arc_lengths[:, 1:2]
    slot_index = jnp.arange(CAP, dtype=jnp.int32)[None, :]
    position = jnp.where(slot_index < first_arc, slot_index, slot_index - first_arc).reshape(-1)
    occupied = (slot_index < filled).reshape(-1)
    whitened = jnp.zeros_like(design)
    for lag_index in range(LAGS):
        shifted = jnp.pad(design, ((lag_index, 0), (0, 0)))[:SLOTS]
        weight_mask = (occupied & (position >= lag_index)).astype(jnp.float32)[:, None]
        whitened = whitened + filter_band[:, lag_index:lag_index + 1] * weight_mask * shifted
    destination = jnp.where(occupied, jnp.cumsum(occupied.astype(jnp.int32)) - 1, OBS).astype(jnp.int32)
    packed = jnp.zeros((OBS, P_SIZE), jnp.float32).at[destination].set(whitened, mode="drop")
    normal = lax.dot_general(packed, packed, (((0,), (0,)), ((), ())), precision=lax.Precision.HIGHEST, preferred_element_type=jnp.float32)
    return normal / OBS
```

```python
import jax
import jax.numpy as jnp
from jax import lax
from jax.experimental import pallas as pl
from jax.experimental.pallas import tpu as pltpu
from jax.sharding import PartitionSpec as P

LIVE = 896
LANES = 128
SLAB = 192
SLOTS = 12
HALF = SLOTS // 2
PIECE = SLOTS + HALF
BLOCK = 2 * PIECE + 1
AXES = ("row", "col")


def whiten_kernel(arcs, taps, design, out):
    first = arcs[0, 0]
    filled = first + arcs[0, 1]
    lag_count = taps.shape[1]
    row = lax.broadcasted_iota(jnp.int32, (SLOTS, lag_count), 0)
    lag = lax.broadcasted_iota(jnp.int32, (SLOTS, lag_count), 1)
    position = jnp.where(row < first, row, row - first)
    weights = jnp.where((row < filled) & (position >= lag), taps[...], 0.0)
    columns = []
    for source in range(SLOTS):
        picked = jnp.where(row - source == lag, weights, 0.0)
        columns.append(jnp.broadcast_to(jnp.sum(picked, axis=1, keepdims=True), (SLOTS, LANES)))
    low_lanes = lax.broadcasted_iota(jnp.int32, (HALF, LANES), 1) < LANES // 2

    def tile(start):
        total = columns[0] * design[pl.ds(0, 1), pl.ds(start, LANES)]
        for source in range(1, SLOTS):
            total = total + columns[source] * design[pl.ds(source, 1), pl.ds(start, LANES)]
        return total

    def pair(index, carry):
        start = index * (3 * LANES)
        left, middle, right = (tile(pl.multiple_of(start + k * LANES, LANES)) for k in range(3))
        upper, lower = middle[:HALF], middle[HALF:]
        even = jnp.where(low_lanes, upper, pltpu.roll(lower, LANES // 2, 1))
        odd = jnp.where(low_lanes, pltpu.roll(upper, LANES // 2, 1), lower)
        for parity, whole, part in ((0, left, even), (1, right, odd)):
            slab = 2 * index + parity
            right_at = ((slab % 16) * 8 + slab // 16) * BLOCK
            left_at = slab * BLOCK + PIECE
            for at in (right_at, left_at):
                out[pl.ds(at, SLOTS), :] = whole
                out[pl.ds(at + SLOTS, HALF), :] = part
        return carry

    lax.fori_loop(0, design.shape[1] // (3 * LANES), pair, 0)
    devices = out.shape[0] // BLOCK
    out[pl.ds(2 * PIECE, devices, stride=BLOCK), :] = jnp.full((devices, LANES), filled, jnp.int32).astype(jnp.float32)


def split(value):
    high = value.astype(jnp.bfloat16)
    return high, (value - high.astype(jnp.float32)).astype(jnp.bfloat16)


def pack_kernel(offsets, received, right_out, left_out, chosen, high, low):
    devices = received.shape[0] // BLOCK
    count = received[pl.ds(2 * PIECE, devices, stride=BLOCK), :]
    later = lax.broadcasted_iota(jnp.int32, (devices, devices), 0) > lax.broadcasted_iota(jnp.int32, (devices, devices), 1)
    start = jnp.dot(later.astype(jnp.bfloat16), count.astype(jnp.bfloat16), preferred_element_type=jnp.float32)
    lane = lax.broadcasted_iota(jnp.int32, (devices, LANES), 1)
    low_lanes = lane < LANES // 2
    lane = lane.astype(jnp.float32)
    for slot in range(SLOTS):
        rows = pl.ds(slot * devices, devices)
        target = jnp.where(count > slot, start + slot, -1.0)
        for group in range(LIVE // LANES):
            chosen[rows, pl.ds(group * LANES, LANES)] = (target - group * LANES == lane).astype(jnp.bfloat16)
        whole = [received[pl.ds(base + slot, devices, stride=BLOCK), :] for base in (0, PIECE)]
        right_part, left_part = (received[pl.ds(base + SLOTS + slot % HALF, devices, stride=BLOCK), :] for base in (0, PIECE))
        if slot < HALF:
            part = jnp.where(low_lanes, right_part, pltpu.roll(left_part, LANES // 2, 1))
        else:
            part = jnp.where(low_lanes, pltpu.roll(right_part, LANES // 2, 1), left_part)
        for index, value in enumerate((*whole, part)):
            high[rows, pl.ds(index * LANES, LANES)], low[rows, pl.ds(index * LANES, LANES)] = split(value)
    contract = (((0,), (0,)), ((), ()))
    packed = lax.dot_general(high[...], chosen[...], contract, preferred_element_type=jnp.float32)
    packed += lax.dot_general(low[...], chosen[...], contract, preferred_element_type=jnp.float32)
    for which, out in enumerate((right_out, left_out)):
        odd = offsets[which]
        out[pl.ds(pl.multiple_of(odd * (LANES // 2), LANES // 2), LANES), :] = packed[which * LANES : (which + 1) * LANES]
        part_at = pl.multiple_of((1 - odd) * LANES, LANES)
        out[pl.ds(part_at, LANES // 2), :] = packed[2 * LANES + which * (LANES // 2) : 2 * LANES + (which + 1) * (LANES // 2)]


def vmem(count):
    return [pl.BlockSpec(memory_space=pltpu.VMEM)] * count


def gram_kernel(left, right, out, turned, left_parts):
    @pl.when(pl.program_id(0) == 0)
    def _():
        high, low = split(left[...])
        left_parts[:, 0:LIVE] = high
        left_parts[:, LIVE : 2 * LIVE] = high
        left_parts[:, 2 * LIVE :] = low

    for group in range(right.shape[0] // LANES):
        rows, lanes = pl.ds(group * LANES, LANES), pl.ds(group * LANES, LANES)
        high, low = split(right[rows, :].T)
        turned[0:LIVE, lanes] = high
        turned[LIVE : 2 * LIVE, lanes] = low
        turned[2 * LIVE :, lanes] = high

    def rows_of(index, carry):
        rows = pl.ds(pl.multiple_of(index * 256, 256), 256)
        out[rows, :] = jnp.dot(left_parts[rows, :], turned[...], preferred_element_type=jnp.float32) * (1.0 / LIVE)
        return carry

    lax.fori_loop(0, left.shape[0] // 256, rows_of, 0)


def whiten(arcs, taps, design):
    return pl.pallas_call(
        whiten_kernel,
        out_shape=jax.ShapeDtypeStruct((128 * BLOCK, LANES), jnp.float32),
        in_specs=[pl.BlockSpec(memory_space=pltpu.SMEM)] + vmem(2),
        out_specs=vmem(1)[0],
        name="whiten",
    )(arcs, taps, design)


def pack(offsets, received):
    slab = jax.ShapeDtypeStruct((SLAB, LIVE), jnp.float32)
    slots = 128 * SLOTS
    return pl.pallas_call(
        pack_kernel,
        out_shape=(slab, slab),
        in_specs=[pl.BlockSpec(memory_space=pltpu.SMEM)] + vmem(1),
        out_specs=tuple(vmem(2)),
        scratch_shapes=[pltpu.VMEM((slots, LIVE), jnp.bfloat16), pltpu.VMEM((slots, 3 * LANES), jnp.bfloat16), pltpu.VMEM((slots, 3 * LANES), jnp.bfloat16)],
        name="pack",
    )(offsets, received)


def gram(left, right):
    rows, columns, width = left.shape[0], right.shape[0], 768
    return pl.pallas_call(
        gram_kernel,
        out_shape=jax.ShapeDtypeStruct((rows, columns), jnp.float32),
        grid=(columns // width,),
        in_specs=[pl.BlockSpec((rows, LIVE), lambda j: (0, 0)), pl.BlockSpec((width, LIVE), lambda j: (j, 0))],
        out_specs=pl.BlockSpec((rows, width), lambda j: (0, j)),
        scratch_shapes=[pltpu.VMEM((3 * LIVE, width), jnp.bfloat16), pltpu.VMEM((rows, 3 * LIVE), jnp.bfloat16)],
        compiler_params=pltpu.CompilerParams(vmem_limit_bytes=60 << 20),
        name="gram",
    )(left, right)


def exchange(value):
    return lax.all_to_all(value.reshape(128, BLOCK, 1, LANES), AXES, split_axis=0, concat_axis=0, tiled=True).reshape(128 * BLOCK, LANES)


def device(row, col):
    return row * 8 + col


def moves(change):
    return [(device(r, c), device(*change(r, c))) for r in range(16) for c in range(8)]


X = {d: moves(lambda r, c, d=d: ((r + 4 * d) % 16, c)) for d in (1, -1)}
Z_LOW = moves(lambda r, c: (r ^ 2, c))
CORE = moves(lambda r, c: (r ^ 1, c))
Y = {d: moves(lambda r, c, d=d: (r, c // 4 * 4 + (c + d) % 4)) for d in (1, -1)}
Z_HIGH = moves(lambda r, c: (r, c ^ 4))


def send(value, pairs):
    return lax.ppermute(value, AXES, pairs)


def ring(own, forward, backward, across):
    before, after = send(own, forward), send(own, backward)
    other = send(own, across)
    other_before, other_after = send(other, forward), send(other, backward)
    far, other_far = send(before, forward), send(other_after, backward)
    return (own, before, far, after), (other, other_before, other_far, other_after)


def assemble_left(slabs, col):
    (own, before, far, after), (other, obefore, ofar, oafter) = slabs
    y = col % 4
    hi = col // 4
    mine = jnp.concatenate([own, before, far, after])
    theirs = jnp.concatenate([other, obefore, ofar, oafter])
    def order(a):
        return jnp.concatenate([lax.dynamic_slice_in_dim(a, ((y - p) % 4) * SLAB, SLAB, 0) for p in range(4)])
    mine, theirs = order(mine), order(theirs)
    return jnp.where(hi == 0, jnp.concatenate([mine, theirs]), jnp.concatenate([theirs, mine]))


def shards(design, taps, arcs):
    row, col = lax.axis_index("row"), lax.axis_index("col")
    offsets = jnp.stack([row % 2, col % 2]).astype(jnp.int32)
    right_slab, left_slab = pack(offsets, exchange(whiten(arcs, taps, design)))
    right_panel = lax.all_gather(right_slab, "row", axis=0, tiled=True)
    left_panel = assemble_left(ring(left_slab, Y[1], Y[-1], Z_HIGH), col)
    return gram(left_panel, right_panel)


def solution(mesh):
    placed = P(AXES, None)
    return jax.shard_map(shards, mesh=mesh, in_specs=(placed, placed, placed), out_specs=P("row", "col"), check_vma=False)
```

```python
import functools

import jax
import jax.numpy as jnp
from jax import lax
from jax.experimental import pallas as pl
from jax.experimental.pallas import tpu as pltpu
from jax.sharding import PartitionSpec as P

LIVE = 896
LANES = 128
SLAB = 192
SLOTS = 12
HALF = SLOTS // 2
PIECE = SLOTS + HALF
BLOCK = 2 * PIECE + 1
AXES = ("row", "col")


def whiten_kernel(arcs, taps, design, out):
    first = arcs[0, 0]
    filled = first + arcs[0, 1]
    lag_count = taps.shape[0]
    lag = lax.broadcasted_iota(jnp.int32, (lag_count, SLOTS), 0)
    slot = lax.broadcasted_iota(jnp.int32, (lag_count, SLOTS), 1)
    position = jnp.where(slot < first, slot, slot - first)
    weights = jnp.where((slot < filled) & (position >= lag), taps[...], 0.0)
    diagonal = lax.broadcasted_iota(jnp.int32, (SLOTS, SLOTS), 0) == lax.broadcasted_iota(jnp.int32, (SLOTS, SLOTS), 1)
    columns = []
    for source in range(SLOTS):
        across = jnp.sum(jnp.where(slot - source == lag, weights, 0.0), axis=0, keepdims=True)
        column = jnp.sum(jnp.where(diagonal, across, 0.0), axis=1, keepdims=True)
        columns.append((jnp.broadcast_to(column[:8], (8, LANES)), jnp.broadcast_to(column[8:], (SLOTS - 8, LANES))))
    low_lanes = lax.broadcasted_iota(jnp.int32, (HALF, LANES), 1) < LANES // 2

    def tile(start):
        rows = [design[pl.ds(source, 1), pl.ds(start, LANES)] for source in range(SLOTS)]
        upper = sum(columns[source][0] * rows[source] for source in range(8))
        lower = sum(columns[source][1] * rows[source] for source in range(9 - lag_count, SLOTS))
        return jnp.concatenate([upper, lower])

    def pair(index, carry):
        start = index * (3 * LANES)
        left, middle, right = (tile(pl.multiple_of(start + k * LANES, LANES)) for k in range(3))
        upper, lower = middle[:HALF], middle[HALF:]
        even = jnp.where(low_lanes, upper, pltpu.roll(lower, LANES // 2, 1))
        odd = jnp.where(low_lanes, pltpu.roll(upper, LANES // 2, 1), lower)
        for parity, whole, part in ((0, left, even), (1, right, odd)):
            slab = 2 * index + parity
            right_at = ((slab % 16) * 8 + slab // 16) * BLOCK
            left_at = slab * BLOCK + PIECE
            for at in (right_at, left_at):
                out[pl.ds(at, SLOTS), :] = whole
                out[pl.ds(at + SLOTS, HALF), :] = part
        return carry

    lax.fori_loop(0, design.shape[1] // (3 * LANES), pair, 0, unroll=4)
    devices = out.shape[0] // BLOCK
    out[pl.ds(2 * PIECE, devices, stride=BLOCK), :] = jnp.full((devices, LANES), filled, jnp.int32).astype(jnp.float32)


def split(value):
    high = value.astype(jnp.bfloat16)
    return high, (value - high.astype(jnp.float32)).astype(jnp.bfloat16)


def pack_kernel(odd, received, right_out, left_out, chosen, high, low):
    devices = received.shape[0] // BLOCK
    count = received[pl.ds(2 * PIECE, devices, stride=BLOCK), :]
    later = lax.broadcasted_iota(jnp.int32, (devices, devices), 0) > lax.broadcasted_iota(jnp.int32, (devices, devices), 1)
    start = jnp.dot(later.astype(jnp.bfloat16), count.astype(jnp.bfloat16), preferred_element_type=jnp.float32)
    count, start = count.T, start.T
    low_lanes = lax.broadcasted_iota(jnp.int32, (devices, LANES), 1) < LANES // 2
    place = lax.broadcasted_iota(jnp.int32, (LANES, devices), 0).astype(jnp.float32)
    for slot in range(SLOTS):
        rows = pl.ds(slot * devices, devices)
        target = jnp.where(count > slot, start + slot, -1.0)
        for group in range(LIVE // LANES):
            chosen[pl.ds(group * LANES, LANES), rows] = (target - group * LANES == place).astype(jnp.bfloat16)
        whole = [received[pl.ds(base + slot, devices, stride=BLOCK), :] for base in (0, PIECE)]
        right_part, left_part = (received[pl.ds(base + SLOTS + slot % HALF, devices, stride=BLOCK), :] for base in (0, PIECE))
        if slot < HALF:
            part = jnp.where(low_lanes, right_part, pltpu.roll(left_part, LANES // 2, 1))
        else:
            part = jnp.where(low_lanes, pltpu.roll(right_part, LANES // 2, 1), left_part)
        for index, value in enumerate((*whole, part)):
            high[rows, pl.ds(index * LANES, LANES)], low[rows, pl.ds(index * LANES, LANES)] = split(value)
    packed = jnp.dot(chosen[...], high[...], preferred_element_type=jnp.float32)
    packed += jnp.dot(chosen[...], low[...], preferred_element_type=jnp.float32)
    part = packed[:, 2 * LANES :]
    right_out[0:LIVE, :] = packed[:, :LANES]
    early, late = part[: LIVE // 2], part[LIVE // 2 :]
    even = jnp.where(jnp.tile(low_lanes[:64], (LIVE // 128, 1)), early, pltpu.roll(late, LANES // 2, 1))
    right_out[LIVE:, :] = jnp.where(odd[0] == 1, pltpu.roll(even, LANES // 2, 1), even)
    left_out[pl.ds(pl.multiple_of(odd[1] * (LANES // 2), LANES // 2), LANES), :] = packed[:, LANES : 2 * LANES].T
    left_out[pl.ds(pl.multiple_of((1 - odd[1]) * LANES, LANES), LANES // 2), :] = part.T[LANES // 2 :]


def vmem(count):
    return [pl.BlockSpec(memory_space=pltpu.VMEM)] * count


WIDE = 4 * SLAB
PAIR = 2 * SLAB
PACKED = LIVE + LIVE // 2
CHUNKS = 4


def chunks_of(first, count):
    return [(first + at, min(2, count - at)) for at in range(0, count, 2)]


def gram_kernel(plan, left_count, fresh_count, ready_count, emitted, sided, where, *refs):
    left_refs, refs = refs[:left_count], refs[left_count:]
    fresh_refs, refs = refs[: 4 * fresh_count], refs[4 * fresh_count :]
    ready_refs, refs = refs[:ready_count], refs[ready_count + sided :]
    out, refs = refs[0], refs[1:]
    emit_refs, refs = refs[:emitted], refs[emitted:]
    left_f, left_parts, right_f, right_parts, stage, left_sem, right_sem, ready_sem, emit_sem, out_sem = refs
    left_copies = [pltpu.make_async_copy(ref, left_f.at[pl.ds(i * SLAB, SLAB)], left_sem.at[i]) for i, ref in enumerate(left_refs)]
    fresh_copies = [pltpu.make_async_copy(ref, right_f.at[i // 4, where[24 + i % 4]], right_sem.at[i]) for i, ref in enumerate(fresh_refs)]
    half = LANES // 2
    low_lanes = lax.broadcasted_iota(jnp.int32, (half, LANES), 1) < half

    def ready_copy(turn):
        index = plan[turn][0] - fresh_count
        return pltpu.make_async_copy(ready_refs[index], right_parts.at[turn % 2], ready_sem.at[index])

    def emit_copy(turn):
        group = plan[turn][0]
        return pltpu.make_async_copy(right_parts.at[turn % 2], emit_refs[group], emit_sem.at[group])

    def is_fresh(turn):
        return plan[turn][0] < fresh_count

    def emits(turn):
        return plan[turn][0] < emitted

    def fetch(turn):
        if is_fresh(turn):
            for copy in fresh_copies[4 * plan[turn][0] : 4 * plan[turn][0] + 4]:
                copy.start()
        elif turn < 2:
            ready_copy(turn).start()

    needed = []
    for _, first, count in plan:
        needed += [index for index in range(first, first + count) if index not in needed]
    fetch(0)
    for index in needed:
        left_copies[index].start()
    for turn in range(1, len(plan)):
        fetch(turn)

    def split_left(index):
        left_copies[index].wait()
        rows = pl.ds(index * SLAB, SLAB)
        high, low = split(left_f[rows, :])
        left_parts[rows, 0:LIVE] = high
        left_parts[rows, LIVE : 2 * LIVE] = high
        left_parts[rows, 2 * LIVE :] = low

    def out_copy(slot, part, side, at, column):
        source = stage.at[slot, pl.ds(part * SLAB, SLAB), pl.ds(side * PAIR, PAIR)]
        return pltpu.make_async_copy(source, out.at[pl.ds(at, SLAB), pl.ds(column, PAIR)], out_sem.at[slot, part, side])

    def wait_stage(turn):
        for index, (_, size) in enumerate(chunks_of(*plan[turn][1:])):
            for part in range(size):
                for side in (0, 1):
                    out_copy((turn % 2) * CHUNKS + index, part, side, 0, 0).wait()

    done = set()
    for turn, (group, first, count) in enumerate(plan):
        buffer = right_parts.at[turn % 2]
        if turn >= 2:
            wait_stage(turn - 2)
        if is_fresh(turn):
            for copy in fresh_copies[4 * group : 4 * group + 4]:
                copy.wait()
            if turn >= 2 and emits(turn - 2):
                emit_copy(turn - 2).wait()

            def split_right(index, carry):
                for side in (0, 1):
                    even, odd = right_f.at[group, 2 * side], right_f.at[group, 2 * side + 1]
                    rows, later = pl.ds(pl.multiple_of(index * half, half), half), pl.ds(pl.multiple_of(LIVE // 2 + index * half, half), half)
                    parts = pl.ds(pl.multiple_of(LIVE + index * half, half), half)
                    one, two = even[parts, :], odd[parts, :]
                    middle = jnp.where(low_lanes, one, two)
                    crossed = pltpu.roll(jnp.where(low_lanes, two, one), half, 1)
                    for tile, (value, after) in enumerate(((even[rows, :], even[later, :]), (middle, crossed), (odd[rows, :], odd[later, :]))):
                        lanes = pl.ds((3 * side + tile) * LANES, LANES)
                        for offset, block in ((0, value), (LIVE // 2, after)):
                            high, low = split(block)
                            for base, piece in ((0, high), (LIVE, low), (2 * LIVE, high)):
                                buffer[pl.ds(pl.multiple_of(base + offset + index * half, half), half), lanes] = piece
                return carry

            lax.fori_loop(0, LIVE // LANES, split_right, 0)
            if emits(turn):
                emit_copy(turn).start()
        else:
            ready_copy(turn).wait()
        if 1 <= turn < len(plan) - 1 and not is_fresh(turn + 1):
            if emits(turn - 1):
                emit_copy(turn - 1).wait()
            ready_copy(turn + 1).start()

        def rows_of(index, begin, size):
            slot = (turn % 2) * CHUNKS + index
            begin = pl.multiple_of(begin * SLAB, SLAB)
            stage[slot, 0 : size * SLAB] = jnp.dot(left_parts[pl.ds(begin, size * SLAB), :], buffer[...], preferred_element_type=jnp.float32) * (1.0 / LIVE)

        def put(index, begin, size):
            for part in range(size):
                at = pl.multiple_of(where[begin + part] * SLAB, SLAB)
                for side in (0, 1):
                    column = pl.multiple_of(where[12 + 2 * group + side] * PAIR, PAIR)
                    out_copy((turn % 2) * CHUNKS + index, part, side, at, column).start()

        chunks = chunks_of(first, count)
        fresh = [index for index in range(first, first + count) if index not in done]
        if turn == 0:
            for index, (begin, size) in enumerate(chunks):
                for at in range(begin, begin + size):
                    split_left(at)
                rows_of(index, begin, size)
                put(index, begin, size)
        else:
            for at in fresh:
                split_left(at)

            def body(index, carry):
                rows_of(index, first + 2 * index, 2)
                put(index, first + 2 * index, 2)
                return carry

            lax.fori_loop(0, count // 2, body, 0)
            if count % 2:
                rows_of(count // 2, *chunks[-1])
                put(count // 2, *chunks[-1])
        done.update(range(first, first + count))
    for turn in range(max(0, len(plan) - 2), len(plan)):
        if emits(turn):
            emit_copy(turn).wait()
        wait_stage(turn)


def gram(plan, lefts, left_at, fresh, ready, right_at, slots, emitted, out):
    fill = jnp.zeros((), jnp.int32)
    where = jnp.stack([*left_at, *[fill] * (12 - len(lefts)), *right_at, *[fill] * (12 - len(right_at)), *slots])
    operands = [*lefts, *[slab for group in fresh for slab in group], *ready]
    blocks = sum(count for _, _, count in plan)
    sided = int(out is not None)
    specs = [pl.BlockSpec(memory_space=pltpu.SMEM)] + [pl.BlockSpec(memory_space=pl.ANY)] * (len(operands) + sided)
    aliases = {len(operands) + 1: 0} if sided else {}
    if sided:
        operands.append(out)
    parts = jax.ShapeDtypeStruct((3 * LIVE, WIDE), jnp.bfloat16)
    return pl.pallas_call(
        functools.partial(gram_kernel, plan, len(lefts), len(fresh), len(ready), emitted, sided),
        out_shape=(jax.ShapeDtypeStruct((1536, 3072), jnp.float32), *[parts] * emitted),
        in_specs=specs,
        out_specs=(pl.BlockSpec(memory_space=pl.ANY),) * (1 + emitted),
        scratch_shapes=[
            pltpu.VMEM((len(lefts) * SLAB, LIVE), jnp.float32),
            pltpu.VMEM((len(lefts) * SLAB, 3 * LIVE), jnp.bfloat16),
            pltpu.VMEM((len(fresh), 4, PACKED, LANES), jnp.float32),
            pltpu.VMEM((2, 3 * LIVE, WIDE), jnp.bfloat16),
            pltpu.VMEM((2 * CHUNKS, PAIR, WIDE), jnp.float32),
            pltpu.SemaphoreType.DMA((len(lefts),)),
            pltpu.SemaphoreType.DMA((4 * len(fresh),)),
            pltpu.SemaphoreType.DMA((max(1, len(ready)),)),
            pltpu.SemaphoreType.DMA((max(1, emitted),)),
            pltpu.SemaphoreType.DMA((2 * CHUNKS, 2, 2)),
        ],
        input_output_aliases=aliases,
        compiler_params=pltpu.CompilerParams(vmem_limit_bytes=52 << 20),
        cost_estimate=pl.CostEstimate(flops=2 * SLAB * WIDE * 3 * LIVE * blocks, bytes_accessed=4 * SLAB * WIDE * blocks, transcendentals=0),
    )(where, *operands)


def whiten(arcs, taps, design):
    return pl.pallas_call(
        whiten_kernel,
        out_shape=jax.ShapeDtypeStruct((128 * BLOCK, LANES), jnp.float32),
        in_specs=[pl.BlockSpec(memory_space=pltpu.SMEM)] + vmem(2),
        out_specs=vmem(1)[0],
        name="whiten",
    )(arcs, taps.T, design)


def pack(odd, received):
    slots = 128 * SLOTS
    return pl.pallas_call(
        pack_kernel,
        out_shape=(jax.ShapeDtypeStruct((PACKED, LANES), jnp.float32), jax.ShapeDtypeStruct((SLAB, LIVE), jnp.float32)),
        in_specs=[pl.BlockSpec(memory_space=pltpu.SMEM)] + vmem(1),
        out_specs=tuple(vmem(2)),
        scratch_shapes=[pltpu.VMEM((LIVE, slots), jnp.bfloat16), pltpu.VMEM((slots, 3 * LANES), jnp.bfloat16), pltpu.VMEM((slots, 3 * LANES), jnp.bfloat16)],
        compiler_params=pltpu.CompilerParams(vmem_limit_bytes=24 << 20),
        name="pack",
    )(odd, received)


def exchange(value):
    return lax.all_to_all(value.reshape(128, BLOCK, 1, LANES), AXES, split_axis=0, concat_axis=0, tiled=True).reshape(128 * BLOCK, LANES)


def device(row, col):
    return row * 8 + col


def moves(change):
    return [(device(r, c), device(*change(r, c))) for r in range(16) for c in range(8)]


X = {d: moves(lambda r, c, d=d: ((r + 4 * d) % 16, c)) for d in (1, -1)}
Z_LOW = moves(lambda r, c: (r ^ 2, c))
CORE = moves(lambda r, c: (r ^ 1, c))
Y = {d: moves(lambda r, c, d=d: (r, c // 4 * 4 + (c + d) % 4)) for d in (1, -1)}
Z_HIGH = moves(lambda r, c: (r, c ^ 4))


def send(value, pairs):
    return lax.ppermute(value, AXES, pairs)


def right_ring(own):
    other = send(own, Z_LOW)
    before, after = send(own, X[1]), send(own, X[-1])
    other_before, other_after = send(other, X[1]), send(other, X[-1])
    far, other_far = send(before, X[1]), send(other_after, X[-1])
    return {(0, 0): own, (0, 1): other, (-1, 0): before, (1, 0): after, (-1, 1): other_before, (1, 1): other_after, (2, 0): far, (2, 1): other_far}


def left_ring(own):
    other = send(own, Z_HIGH)
    before, after = send(own, Y[1]), send(own, Y[-1])
    far = send(before, Y[1])
    other_before, other_after, other_far = send(other, Y[1]), send(other, Y[-1]), send(far, Z_HIGH)
    return {(0, 0): own, (0, 1): other, (-1, 0): before, (1, 0): after, (-1, 1): other_before, (1, 1): other_after, (2, 0): far, (2, 1): other_far}


LEFT_ORDER = ((0, 0), (-1, 0), (1, 0), (0, 1), (2, 0), (-1, 1), (1, 1), (2, 1))
RIGHT_ORDER = ((0, 0), (0, 1), (-1, 0), (1, 0), (-1, 1), (1, 1), (2, 0), (2, 1))


def assemble(design, taps, arcs):
    row, col = lax.axis_index("row"), lax.axis_index("col")
    odd = jnp.stack([row % 2, col % 2]).astype(jnp.int32)
    right, left = pack(odd, exchange(whiten(arcs, taps, design)))
    rights, lefts = right_ring(right), left_ring(left)
    siblings = {key: send(rights[key], CORE) for key in RIGHT_ORDER}
    x, y, high, side, core = row // 4, col % 4, col // 4, row // 2 % 2, row % 2
    groups = [tuple(slab for key in RIGHT_ORDER[i : i + 2] for slab in (rights[key], siblings[key])) for i in range(0, 8, 2)]
    right_at = [(x + step) % 4 * 2 + (side + other) % 2 for step, other in RIGHT_ORDER]
    left_at = [(high + other) % 2 * 4 + (y + step) % 4 for step, other in LEFT_ORDER]
    lefts = [lefts[key] for key in LEFT_ORDER]
    slots = [core, 1 - core, 2 + core, 3 - core]
    out, one, two = gram(((0, 0, 3), (1, 0, 3)), lefts[:3], left_at[:3], groups[:2], [], right_at[:4], slots, 2, None)
    out, three = gram(((1, 3, 2), (2, 3, 2), (0, 0, 5)), lefts[:5], left_at[:5], groups[2:3], [one, two], right_at[4:6] + right_at[:4], slots, 1, out)
    return gram(((1, 5, 3), (2, 5, 3), (3, 5, 3), (0, 0, 8)), lefts, left_at, groups[3:], [one, two, three], right_at[6:] + right_at[:6], slots, 0, out)[0]


def solution(mesh):
    placed = P(AXES, None)
    return jax.shard_map(assemble, mesh=mesh, in_specs=(placed, placed, placed), out_specs=P("row", "col"), check_vma=False)
```

```python
import functools

import jax
import jax.numpy as jnp
from jax import lax
from jax.experimental import pallas as pl
from jax.experimental.pallas import tpu as pltpu
from jax.sharding import PartitionSpec as P

LIVE = 896
LANES = 128
SLAB = 192
SLOTS = 12
HALF = SLOTS // 2
PIECE = SLOTS + HALF
BLOCK = 2 * PIECE + 1
AXES = ("row", "col")


def whiten_kernel(arcs, taps, design, out):
    first = arcs[0, 0]
    filled = first + arcs[0, 1]
    lag_count = taps.shape[0]
    lag = lax.broadcasted_iota(jnp.int32, (lag_count, SLOTS), 0)
    slot = lax.broadcasted_iota(jnp.int32, (lag_count, SLOTS), 1)
    position = jnp.where(slot < first, slot, slot - first)
    weights = jnp.where((slot < filled) & (position >= lag), taps[...], 0.0)
    diagonal = lax.broadcasted_iota(jnp.int32, (SLOTS, SLOTS), 0) == lax.broadcasted_iota(jnp.int32, (SLOTS, SLOTS), 1)
    columns = []
    for source in range(SLOTS):
        across = jnp.sum(jnp.where(slot - source == lag, weights, 0.0), axis=0, keepdims=True)
        column = jnp.sum(jnp.where(diagonal, across, 0.0), axis=1, keepdims=True)
        columns.append((jnp.broadcast_to(column[:8], (8, LANES)), jnp.broadcast_to(column[8:], (SLOTS - 8, LANES))))
    low_lanes = lax.broadcasted_iota(jnp.int32, (HALF, LANES), 1) < LANES // 2

    def tile(start):
        rows = [design[pl.ds(source, 1), pl.ds(start, LANES)] for source in range(SLOTS)]
        upper = sum(columns[source][0] * rows[source] for source in range(8))
        lower = sum(columns[source][1] * rows[source] for source in range(9 - lag_count, SLOTS))
        return jnp.concatenate([upper, lower])

    def pair(index, carry):
        start = index * (3 * LANES)
        left, middle, right = (tile(pl.multiple_of(start + k * LANES, LANES)) for k in range(3))
        upper, lower = middle[:HALF], middle[HALF:]
        even = jnp.where(low_lanes, upper, pltpu.roll(lower, LANES // 2, 1))
        odd = jnp.where(low_lanes, pltpu.roll(upper, LANES // 2, 1), lower)
        for parity, whole, part in ((0, left, even), (1, right, odd)):
            slab = 2 * index + parity
            right_at = ((slab % 16) * 8 + slab // 16) * BLOCK
            left_at = slab * BLOCK + PIECE
            for at in (right_at, left_at):
                out[pl.ds(at, SLOTS), :] = whole
                out[pl.ds(at + SLOTS, HALF), :] = part
        return carry

    lax.fori_loop(0, design.shape[1] // (3 * LANES), pair, 0, unroll=4)
    devices = out.shape[0] // BLOCK
    out[pl.ds(2 * PIECE, devices, stride=BLOCK), :] = jnp.full((devices, LANES), filled, jnp.int32).astype(jnp.float32)


def split(value):
    high = value.astype(jnp.bfloat16)
    return high, (value - high.astype(jnp.float32)).astype(jnp.bfloat16)


def pack_kernel(odd, received, right_out, left_out, chosen, parts):
    devices = received.shape[0] // BLOCK
    count = received[pl.ds(2 * PIECE, devices, stride=BLOCK), :]
    later = lax.broadcasted_iota(jnp.int32, (devices, devices), 0) > lax.broadcasted_iota(jnp.int32, (devices, devices), 1)
    start = jnp.dot(later.astype(jnp.bfloat16), count.astype(jnp.bfloat16), preferred_element_type=jnp.float32)
    count, start = count.T, start.T
    low_lanes = lax.broadcasted_iota(jnp.int32, (devices, LANES), 1) < LANES // 2
    place = lax.broadcasted_iota(jnp.int32, (LANES, devices), 0).astype(jnp.float32)
    for slot in range(SLOTS):
        rows = pl.ds(slot * devices, devices)
        target = jnp.where(count > slot, start + slot, -1.0)
        for group in range(LIVE // LANES):
            chosen[pl.ds(group * LANES, LANES), rows] = (target - group * LANES == place).astype(jnp.bfloat16)
        whole = [received[pl.ds(base + slot, devices, stride=BLOCK), :] for base in (0, PIECE)]
        right_part, left_part = (received[pl.ds(base + SLOTS + slot % HALF, devices, stride=BLOCK), :] for base in (0, PIECE))
        if slot < HALF:
            part = jnp.where(low_lanes, right_part, pltpu.roll(left_part, LANES // 2, 1))
        else:
            part = jnp.where(low_lanes, pltpu.roll(right_part, LANES // 2, 1), left_part)
        for index, value in enumerate((*whole, part)):
            parts[rows, pl.ds(index * LANES, LANES)], parts[rows, pl.ds((3 + index) * LANES, LANES)] = split(value)
    packed = jnp.dot(chosen[...], parts[...], preferred_element_type=jnp.float32)
    packed = packed[:, : 3 * LANES] + packed[:, 3 * LANES :]
    part = packed[:, 2 * LANES :]
    right_out[0:LIVE, :] = packed[:, :LANES]
    early, late = part[: LIVE // 2], part[LIVE // 2 :]
    even = jnp.where(jnp.tile(low_lanes[:64], (LIVE // 128, 1)), early, pltpu.roll(late, LANES // 2, 1))
    right_out[LIVE:, :] = jnp.where(odd[0] == 1, pltpu.roll(even, LANES // 2, 1), even)
    left_out[pl.ds(pl.multiple_of(odd[1] * (LANES // 2), LANES // 2), LANES), :] = packed[:, LANES : 2 * LANES].T
    left_out[pl.ds(pl.multiple_of((1 - odd[1]) * LANES, LANES), LANES // 2), :] = part.T[LANES // 2 :]


def vmem(count):
    return [pl.BlockSpec(memory_space=pltpu.VMEM)] * count


WIDE = 4 * SLAB
PAIR = 2 * SLAB
PACKED = LIVE + LIVE // 2
TALL = 3
DEEP = 8
STEP = 112


def gram_kernel(plan, left_count, fresh_count, ready_count, emitted, sided, where, *refs):
    left_refs, refs = refs[:left_count], refs[left_count:]
    fresh_refs, refs = refs[: 4 * fresh_count], refs[4 * fresh_count :]
    ready_refs, refs = refs[:ready_count], refs[ready_count + sided :]
    out, refs = refs[0], refs[1:]
    emit_refs, refs = refs[:emitted], refs[emitted:]
    left_f, left_parts, right_f, right_parts, stage, left_sem, right_sem, ready_sem, emit_sem, out_sem = refs
    left_copies = [pltpu.make_async_copy(ref, left_f.at[pl.ds(i * SLAB, SLAB)], left_sem.at[i]) for i, ref in enumerate(left_refs)]
    fresh_copies = [pltpu.make_async_copy(ref, right_f.at[i // 4, where[24 + i % 4]], right_sem.at[i]) for i, ref in enumerate(fresh_refs)]
    half = LANES // 2
    low_lanes = lax.broadcasted_iota(jnp.int32, (STEP, LANES), 1) < half

    def ready_copy(turn):
        index = plan[turn][0] - fresh_count
        return pltpu.make_async_copy(ready_refs[index], right_parts.at[turn % 2], ready_sem.at[index])

    def emit_copy(turn):
        group = plan[turn][0]
        return pltpu.make_async_copy(right_parts.at[turn % 2], emit_refs[group], emit_sem.at[group])

    def is_fresh(turn):
        return plan[turn][0] < fresh_count

    def emits(turn):
        return plan[turn][0] < emitted

    def fetch(turn):
        if is_fresh(turn):
            for copy in fresh_copies[4 * plan[turn][0] : 4 * plan[turn][0] + 4]:
                copy.start()
        elif turn < 2:
            ready_copy(turn).start()

    needed = []
    for _, first, count in plan:
        needed += [index for index in range(first, first + count) if index not in needed]
    early = 0 if is_fresh(0) else plan[0][2]
    for index in needed[:early]:
        left_copies[index].start()
    fetch(0)
    for index in needed[early:]:
        left_copies[index].start()
    for turn in range(1, len(plan)):
        fetch(turn)

    def split_left(index):
        left_copies[index].wait()
        rows = pl.ds(index * SLAB, SLAB)
        high, low = split(left_f[rows, :])
        left_parts[rows, 0:LIVE] = high
        left_parts[rows, LIVE : 2 * LIVE] = high
        left_parts[rows, 2 * LIVE :] = low

    def out_copy(turn, index, side, at, column):
        source = stage.at[turn % 2, pl.ds(index * SLAB, SLAB), pl.ds(side * PAIR, PAIR)]
        return pltpu.make_async_copy(source, out.at[pl.ds(at, SLAB), pl.ds(column, PAIR)], out_sem.at[turn % 2, index, side])

    def wait_stage(turn):
        for index in range(plan[turn][2]):
            for side in (0, 1):
                out_copy(turn, index, side, 0, 0).wait()

    def convert(turn, inline):
        group = plan[turn][0]
        buffer = right_parts.at[turn % 2]
        for copy in fresh_copies[4 * group : 4 * group + 4]:
            copy.wait()
        if turn >= 2 and emits(turn - 2):
            emit_copy(turn - 2).wait()

        def piece_of(index, carry):
            for side in (0, 1):
                even, odd = right_f.at[group, 2 * side], right_f.at[group, 2 * side + 1]
                rows, later, parts = (pl.ds(pl.multiple_of(start + index * STEP, 16), STEP) for start in (0, LIVE // 2, LIVE))
                one, two = even[parts, :], odd[parts, :]
                middle = jnp.where(low_lanes, one, two)
                crossed = pltpu.roll(jnp.where(low_lanes, two, one), half, 1)
                for tile, (value, after) in enumerate(((even[rows, :], even[later, :]), (middle, crossed), (odd[rows, :], odd[later, :]))):
                    lanes = pl.ds((3 * side + tile) * LANES, LANES)
                    for offset, block in ((0, value), (LIVE // 2, after)):
                        high, low = split(block)
                        for base, piece in ((0, high), (LIVE, low), (2 * LIVE, high)):
                            buffer[pl.ds(pl.multiple_of(base + offset + index * STEP, 16), STEP), lanes] = piece
            return carry

        if inline:
            for index in range(LIVE // 2 // STEP):
                piece_of(index, 0)
        else:
            lax.fori_loop(0, LIVE // 2 // STEP, piece_of, 0)

    done = set()
    for turn, (group, first, count) in enumerate(plan):
        buffer = right_parts.at[turn % 2]
        if turn >= 2:
            wait_stage(turn - 2)
        for index in range(first, first + count):
            if index not in done and not (turn == 0 and is_fresh(0)):
                split_left(index)
        if is_fresh(turn):
            if turn == 0:
                convert(turn, False)
                if emits(turn):
                    emit_copy(turn).start()
        else:
            ready_copy(turn).wait()
        if 1 <= turn < len(plan) - 1 and not is_fresh(turn + 1):
            if emits(turn - 1):
                emit_copy(turn - 1).wait()
            ready_copy(turn + 1).start()

        def rows_of(at, size):
            rows, into = (pl.ds(pl.multiple_of(start * SLAB, SLAB), size * SLAB) for start in (first + at, at))
            product = jnp.dot(left_parts[rows, :], buffer[...], preferred_element_type=jnp.float32)
            stage[turn % 2, into, :] = product * (1.0 / LIVE)
            for index in range(size):
                row = pl.multiple_of(where[first + at + index] * SLAB, SLAB)
                for side in (0, 1):
                    column = pl.multiple_of(where[12 + 2 * group + side] * PAIR, PAIR)
                    out_copy(turn, at + index, side, row, column).start()

        for index in range(first, first + count):
            if turn == 0 and is_fresh(0):
                split_left(index)
        done.update(range(first, first + count))
        if turn + 1 < len(plan):
            if is_fresh(turn + 1):
                convert(turn + 1, True)
            for index in range(plan[turn + 1][1], sum(plan[turn + 1][1:])):
                if index not in done:
                    split_left(index)
                    done.add(index)
        whole = count // TALL
        if whole == 1:
            rows_of(0, TALL)
        elif whole:

            def body(index, carry):
                rows_of(index * TALL, TALL)
                return carry

            lax.fori_loop(0, whole, body, 0)
        if count % TALL:
            rows_of(whole * TALL, count % TALL)
        if turn + 1 < len(plan) and is_fresh(turn + 1) and emits(turn + 1):
            emit_copy(turn + 1).start()
    for turn in range(max(0, len(plan) - 2), len(plan)):
        if emits(turn):
            emit_copy(turn).wait()
        wait_stage(turn)


def gram(plan, lefts, left_at, fresh, ready, right_at, slots, emitted, out):
    fill = jnp.zeros((), jnp.int32)
    where = jnp.stack([*left_at, *[fill] * (12 - len(lefts)), *right_at, *[fill] * (12 - len(right_at)), *slots])
    operands = [*lefts, *[slab for group in fresh for slab in group], *ready]
    blocks = sum(count for _, _, count in plan)
    sided = int(out is not None)
    specs = [pl.BlockSpec(memory_space=pltpu.SMEM)] + [pl.BlockSpec(memory_space=pl.ANY)] * (len(operands) + sided)
    aliases = {len(operands) + 1: 0} if sided else {}
    if sided:
        operands.append(out)
    parts = jax.ShapeDtypeStruct((3 * LIVE, WIDE), jnp.bfloat16)
    return pl.pallas_call(
        functools.partial(gram_kernel, plan, len(lefts), len(fresh), len(ready), emitted, sided),
        out_shape=(jax.ShapeDtypeStruct((1536, 3072), jnp.float32), *[parts] * emitted),
        in_specs=specs,
        out_specs=(pl.BlockSpec(memory_space=pl.ANY),) * (1 + emitted),
        scratch_shapes=[
            pltpu.VMEM((len(lefts) * SLAB, LIVE), jnp.float32),
            pltpu.VMEM((len(lefts) * SLAB, 3 * LIVE), jnp.bfloat16),
            pltpu.VMEM((len(fresh), 4, PACKED, LANES), jnp.float32),
            pltpu.VMEM((2, 3 * LIVE, WIDE), jnp.bfloat16),
            pltpu.VMEM((2, DEEP * SLAB, WIDE), jnp.float32),
            pltpu.SemaphoreType.DMA((len(lefts),)),
            pltpu.SemaphoreType.DMA((4 * len(fresh),)),
            pltpu.SemaphoreType.DMA((max(1, len(ready)),)),
            pltpu.SemaphoreType.DMA((max(1, emitted),)),
            pltpu.SemaphoreType.DMA((2, DEEP, 2)),
        ],
        input_output_aliases=aliases,
        compiler_params=pltpu.CompilerParams(vmem_limit_bytes=52 << 20),
        cost_estimate=pl.CostEstimate(flops=2 * SLAB * WIDE * 3 * LIVE * blocks, bytes_accessed=4 * SLAB * WIDE * blocks, transcendentals=0),
    )(where, *operands)


def whiten(arcs, taps, design):
    return pl.pallas_call(
        whiten_kernel,
        out_shape=jax.ShapeDtypeStruct((128 * BLOCK, LANES), jnp.float32),
        in_specs=[pl.BlockSpec(memory_space=pltpu.SMEM)] + vmem(2),
        out_specs=vmem(1)[0],
        name="whiten",
    )(arcs, taps.T, design)


def pack(odd, received):
    slots = 128 * SLOTS
    return pl.pallas_call(
        pack_kernel,
        out_shape=(jax.ShapeDtypeStruct((PACKED, LANES), jnp.float32), jax.ShapeDtypeStruct((SLAB, LIVE), jnp.float32)),
        in_specs=[pl.BlockSpec(memory_space=pltpu.SMEM)] + vmem(1),
        out_specs=tuple(vmem(2)),
        scratch_shapes=[pltpu.VMEM((LIVE, slots), jnp.bfloat16), pltpu.VMEM((slots, 6 * LANES), jnp.bfloat16)],
        compiler_params=pltpu.CompilerParams(vmem_limit_bytes=24 << 20),
        name="pack",
    )(odd, received)


def exchange(value):
    return lax.all_to_all(value.reshape(128, BLOCK, 1, LANES), AXES, split_axis=0, concat_axis=0, tiled=True).reshape(128 * BLOCK, LANES)


def device(row, col):
    return row * 8 + col


def moves(change):
    return [(device(r, c), device(*change(r, c))) for r in range(16) for c in range(8)]


X = {d: moves(lambda r, c, d=d: ((r + 4 * d) % 16, c)) for d in (1, -1)}
Z_LOW = moves(lambda r, c: (r ^ 2, c))
CORE = moves(lambda r, c: (r ^ 1, c))
Y = {d: moves(lambda r, c, d=d: (r, c // 4 * 4 + (c + d) % 4)) for d in (1, -1)}
Z_HIGH = moves(lambda r, c: (r, c ^ 4))


def send(value, pairs):
    return lax.ppermute(value, AXES, pairs)


def right_ring(own):
    other = send(own, Z_LOW)
    before, after = send(own, X[1]), send(own, X[-1])
    other_before, other_after = send(other, X[1]), send(other, X[-1])
    far, other_far = send(before, X[1]), send(other_after, X[-1])
    return {(0, 0): own, (0, 1): other, (-1, 0): before, (1, 0): after, (-1, 1): other_before, (1, 1): other_after, (2, 0): far, (2, 1): other_far}


def left_ring(own):
    other = send(own, Z_HIGH)
    before, after = send(own, Y[1]), send(own, Y[-1])
    far = send(before, Y[1])
    other_before, other_after, other_far = send(other, Y[1]), send(other, Y[-1]), send(far, Z_HIGH)
    return {(0, 0): own, (0, 1): other, (-1, 0): before, (1, 0): after, (-1, 1): other_before, (1, 1): other_after, (2, 0): far, (2, 1): other_far}


LEFT_ORDER = ((0, 0), (-1, 0), (1, 0), (0, 1), (2, 0), (-1, 1), (1, 1), (2, 1))
RIGHT_ORDER = ((0, 0), (0, 1), (-1, 0), (1, 0), (-1, 1), (1, 1), (2, 0), (2, 1))


def assemble(design, taps, arcs):
    row, col = lax.axis_index("row"), lax.axis_index("col")
    odd = jnp.stack([row % 2, col % 2]).astype(jnp.int32)
    right, left = pack(odd, exchange(whiten(arcs, taps, design)))
    rights, lefts = right_ring(right), left_ring(left)
    siblings = {key: send(rights[key], CORE) for key in RIGHT_ORDER}
    x, y, high, side, core = row // 4, col % 4, col // 4, row // 2 % 2, row % 2
    groups = [tuple(slab for key in RIGHT_ORDER[i : i + 2] for slab in (rights[key], siblings[key])) for i in range(0, 8, 2)]
    right_at = [(x + step) % 4 * 2 + (side + other) % 2 for step, other in RIGHT_ORDER]
    left_at = [(high + other) % 2 * 4 + (y + step) % 4 for step, other in LEFT_ORDER]
    lefts = [lefts[key] for key in LEFT_ORDER]
    slots = [core, 1 - core, 2 + core, 3 - core]
    out, one, two = gram(((0, 0, 3), (1, 0, 3)), lefts[:3], left_at[:3], groups[:2], [], right_at[:4], slots, 2, None)
    out, three = gram(((1, 3, 2), (2, 3, 2), (0, 0, 5)), lefts[:5], left_at[:5], groups[2:3], [one, two], right_at[4:6] + right_at[:4], slots, 1, out)
    return gram(((1, 5, 3), (2, 5, 3), (3, 5, 3), (0, 0, 8)), lefts, left_at, groups[3:], [one, two, three], right_at[6:] + right_at[:6], slots, 0, out)[0]


def solution(mesh):
    placed = P(AXES, None)
    return jax.shard_map(assemble, mesh=mesh, in_specs=(placed, placed, placed), out_specs=P("row", "col"), check_vma=False)
```
